32 devices in a mesh: fsdp: 8 (over y, x, core), win: 4 (over z).
Axes of the slice: x: 2, y: 2, z: 4, core: 2. Of those that a mesh axis runs over, the one named last changes fastest.
Arguments:
- tokens: bfloat16 [16384, 2048], P(('fsdp', 'win')), may hold values from -16 to 16
- block_map: int32 [8, 4], P('fsdp'), may hold values from 0 to 3, each once within a row
- shift: int32 [8], P('fsdp'), may hold values from 1 to 2047
- ln_gain: float32 [2048], replicated, may hold values from 0.5 to 1.5
- w_query: bfloat16 [2048, 1024], P('fsdp'), may hold values from -1 to 1
- w_key: bfloat16 [2048, 1024], P('fsdp'), may hold values from -1 to 1
- w_value: bfloat16 [2048, 1024], P('fsdp'), may hold values from -0.125 to 0.125
- w_out: bfloat16 [1024, 2048], P('fsdp'), may hold values from -0.1875 to 0.1875
- logit_scale: float32 [16], replicated, may hold values from 1 to 300
Outputs:
- mixed: bfloat16 [16384, 2048], P(('fsdp', 'win'))
The draws below stay inside these ranges and needn't reach their ends.
All inputs are finite; a program needn't handle non-finite values.
Results may differ from the reference program's by a relative error of at most 0.008.
Values may be sent and summed in bfloat16 or wider, within the bound.
A program may use at most 128 MiB of HBM per device.

```python
import math
import jax
import jax.numpy as jnp
from jax import lax

D = 2048
HEADS = 16
HEAD = 64
TOK_DEV = 512
HD = 1024
WIN = 2048
WINDOWS = 8
TOKENS = 16384
N_WIN = 4


def cluster_index(key):
    member_of = jax.random.randint(jax.random.fold_in(key, 6), (TOKENS,), 0, 8)
    window_of = jnp.arange(TOKENS, dtype=jnp.int32) // WIN
    return window_of * 8 + member_of


def draw_tokens(key, part):
    picked_rows = cluster_index(key)
    protos = jax.random.normal(jax.random.fold_in(key, 5), (WINDOWS * 8, D), jnp.float32)
    jitter = jax.random.normal(jax.random.fold_in(key, 8), (TOKENS, D), jnp.float32)
    base = jnp.take(protos, picked_rows, axis=0) + 0.5 * jitter
    return jnp.clip(base, -6.0, 6.0).astype(jnp.bfloat16)


def query_key_pair(key):
    first = jnp.clip(jax.random.normal(jax.random.fold_in(key, 11), (D, HD), jnp.float32), -5.0, 5.0)
    second = jnp.clip(jax.random.normal(jax.random.fold_in(key, 12), (D, HD), jnp.float32), -5.0, 5.0)
    second = jnp.clip(0.8 * first + 0.6 * second, -5.0, 5.0)
    factor = 1.0 / math.sqrt(D)
    return (jnp.clip(first * factor, -1.0, 1.0), jnp.clip(second * factor, -1.0, 1.0))


def draw_w_query(key, part):
    return query_key_pair(key)[0].astype(jnp.bfloat16)


def draw_w_key(key, part):
    return query_key_pair(key)[1].astype(jnp.bfloat16)


def touch_ends(values, stream_key, low, top_value):
    extent = values.shape
    spot = [jax.random.randint(jax.random.fold_in(stream_key, axis), (), 0, extent[axis]) for axis in range(len(extent))]
    values = values.at[tuple(spot)].set(low)
    longest = extent.index(max(extent))
    spot[longest] = (spot[longest] + 1) % extent[longest]
    return values.at[tuple(spot)].set(top_value)


def steps_of(rng, shape, shards, smallest, high):
    loudness, own = 1.0, jax.random.fold_in(rng, 6)
    for dim, parts in shards:
        draws = jnp.exp(jax.random.uniform(jax.random.fold_in(own, dim), (parts,), jnp.float32, smallest / len(shards), high / len(shards)))
        loudness = loudness * jnp.repeat(draws, shape[dim] // parts).reshape([-1 if axis == dim else 1 for axis in range(len(shape))])
    return loudness


def normal_values(key, extent, scale, reach, pieces=(), kind=jnp.bfloat16):
    drawn = jax.random.normal(key, extent, jnp.float32) * scale
    if len(pieces) > 0:
        drawn = steps_of(key, extent, pieces, -0.22, 0.18) * drawn
    return jnp.clip(drawn, min=-reach, max=reach).astype(kind)


def setup_inputs(seed: int = 0) -> dict:
    key_of = jax.random.split(jax.random.key(seed), 10)
    tokens = draw_tokens(jax.random.fold_in(key_of[9], 71), 0)
    block_map = jax.vmap(lambda own: jax.random.permutation(own, N_WIN))(jax.random.split(key_of[1], WINDOWS)).reshape((WINDOWS, N_WIN)).astype(jnp.int32)
    shift = touch_ends(jax.random.randint(key_of[2], (WINDOWS,), 1, WIN), jax.random.fold_in(key_of[2], 1), 1, WIN - 1).astype(jnp.int32)
    ln_gain = jnp.clip(1.0 + 0.1 * jax.random.normal(key_of[3], (D,), jnp.float32), 0.5, 1.5)
    w_query = draw_w_query(jax.random.fold_in(key_of[9], 71), 0)
    w_key = draw_w_key(jax.random.fold_in(key_of[9], 71), 0)
    w_value = normal_values(key_of[6], (D, HD), D ** -0.5, 0.125, ((0, 8),))
    w_out = normal_values(key_of[7], (HD, D), HD ** -0.5, 0.1875, ((0, 8),))
    logit_scale = jnp.clip(jnp.exp(jax.random.uniform(key_of[8], (HEADS,), jnp.float32, math.log(1.0), math.log(300.0))), 1.0, 300.0)
    return dict(tokens=tokens, block_map=block_map, shift=shift, ln_gain=ln_gain, w_query=w_query, w_key=w_key, w_value=w_value, w_out=w_out, logit_scale=logit_scale)


def layer_norm(resid, gain):
    center = lax.optimization_barrier(jnp.mean(resid, axis=-1, keepdims=True))
    centred = resid - center
    spread = lax.optimization_barrier(jnp.mean(centred * centred, axis=-1, keepdims=True))
    return (centred * lax.rsqrt(spread + 1e-05) * gain).astype(jnp.bfloat16)

def unit_heads(values, head_count):
    split = values.reshape(values.shape[0], head_count, -1)
    scale = lax.rsqrt(lax.optimization_barrier(jnp.sum(split * split, axis=-1, keepdims=True)) + 1e-06)
    return (split * scale).astype(jnp.bfloat16)

def reference(tokens, block_map, shift, ln_gain, w_query, w_key, w_value, w_out, logit_scale):

    def one_window(packed):
        window_x, order_row, offset = packed
        resid = window_x.astype(jnp.float32)
        normed = layer_norm(resid, ln_gain)
        query = jnp.dot(normed, w_query, preferred_element_type=jnp.float32)
        key_full = jnp.dot(normed, w_key, preferred_element_type=jnp.float32)
        value = jnp.dot(normed, w_value, preferred_element_type=jnp.float32).astype(jnp.bfloat16)
        q_unit = unit_heads(query, HEADS).astype(jnp.float32)
        k_unit = unit_heads(key_full, HEADS).astype(jnp.float32)
        value_heads = value.reshape(WIN, HEADS, HEAD).astype(jnp.float32)
        index = jnp.arange(WIN, dtype=jnp.int32)
        position = order_row[index // TOK_DEV] * TOK_DEV + index % TOK_DEV
        region = position >= offset
        allowed = region[:, None] == region[None, :]
        score = jnp.einsum('ihd,jhd->hij', q_unit, k_unit) * logit_scale[:, None, None]
        score = jnp.where(allowed[None], score, -1e+30)
        best = lax.optimization_barrier(jnp.max(score, axis=-1, keepdims=True))
        weight = jnp.where(allowed[None], jnp.exp(score - best), 0.0)
        probs = (weight / lax.optimization_barrier(jnp.sum(weight, axis=-1, keepdims=True))).astype(jnp.bfloat16)
        attended = jnp.einsum('hij,jhd->ihd', probs.astype(jnp.float32), value_heads)
        attended = attended.reshape(WIN, HD).astype(jnp.bfloat16)
        return (resid + jnp.dot(attended, w_out, preferred_element_type=jnp.float32)).astype(jnp.bfloat16)
    windows = tokens.reshape(WINDOWS, WIN, D)
    result = lax.map(one_window, (windows, block_map, shift))
    return result.reshape(TOKENS, D)
```

```python
import functools
import math

import jax
import jax.numpy as jnp
from jax import lax
from jax.experimental import pallas as pl
from jax.experimental.pallas import tpu as pltpu
from jax.sharding import PartitionSpec as P

MESH = pl.DeviceIdType.MESH
LANES = 128
FAR = 1024.0
CHUNKS = 4


def layer_kernel(
    sizes,
    tokens_ref, map_ref, shift_ref, gain_ref, wq_ref, wk_ref, wv_ref, wo_ref, scale_ref,
    out_ref,
    weights, w_out, incoming, normed, sent, held, keys_t, values_1, heads_out, attended, own_meta, peer_meta,
    load_sem, p1_send, p1_recv, p2_send, p2_recv, p3_send, p3_recv,
    swap_send, swap_recv, meta_send, meta_recv, a2a_send, a2a_recv, back_send, back_recv,
):
    rows_a, rows_b, groups, head_size, pairs = sizes
    tok, width = tokens_ref.shape
    rows = wq_ref.shape[0]
    cols = pairs * LANES
    group_heads = cols // head_size
    steps = groups * pairs
    chunks = w_out.shape[0]
    out_tile = w_out.shape[-1]
    total = steps + chunks
    me = lax.axis_index("fsdp")
    mine = lax.axis_index("win")
    chip = me // 2
    at_a = chip // rows_b
    at_b = chip % rows_b
    at_c = me % 2

    depth = groups // 2
    half = mine // depth
    place = mine % depth
    member = at_c * depth + place
    kept = at_c == half
    moved = at_c != half
    partner = (chip * 2 + 1 - at_c, (mine + depth) % groups)

    def device_of_member(m):
        return (chip * 2 + m // depth, half * depth + m % depth)

    def home_of(block):
        return (chip * 2 + half, block)

    def index_of(a, b, c):
        return (a * rows_b + b) * 2 + c

    a_peers = [index_of((at_a + i) % rows_a, at_b, at_c) for i in range(1, rows_a)]
    b_peers = [index_of(at_a, (at_b + i) % rows_b, at_c) for i in range(1, rows_b)]
    c_peer = index_of(at_a, at_b, 1 - at_c)

    barrier = pltpu.get_barrier_semaphore()
    greeted = 0
    for peer in a_peers + b_peers:
        pl.semaphore_signal(barrier, inc=1, device_id=(peer, mine), device_id_type=MESH)
        greeted += 1
    for core in range(2):
        for i in range(groups):
            if core or i:
                other = chip * 2 + (at_c + core) % 2
                pl.semaphore_signal(
                    barrier, inc=1, device_id=(other, (mine + i) % groups), device_id_type=MESH
                )
                greeted += 1

    def pair_of(step):
        return step % (steps // 2) // depth

    def group_of(step):
        return step % depth * depth + (place + 1 - step // (steps // 2)) % depth

    def loads(step):
        if step >= steps:
            chunk = step - steps
            return [
                pltpu.make_async_copy(
                    wo_ref.at[:, pl.ds(chunk * out_tile, out_tile)],
                    w_out.at[chunk, at_a, at_b, at_c],
                    load_sem.at[step, 0],
                )
            ]
        first = group_of(step) * cols + pair_of(step) * LANES
        window = pl.ds(pl.multiple_of(first, LANES), LANES)
        return [
            pltpu.make_async_copy(
                source.at[:, window],
                weights.at[step, at_a, at_b, at_c, :, pl.ds(m * LANES, LANES)],
                load_sem.at[step, m],
            )
            for m, source in enumerate((wq_ref, wk_ref, wv_ref))
        ]

    for step in range(total):
        for copy in loads(step):
            copy.start()
    for block in range(groups):
        first = (map_ref[0, block] * tok - shift_ref[0]).astype(jnp.float32)
        own_meta[block : block + 1, :] = jnp.full((1, tok), first, jnp.float32)
    own_meta[groups:, :] = jnp.zeros((own_meta.shape[0] - groups, tok), jnp.float32)
    pl.semaphore_wait(barrier, greeted)

    quarter = tok // 4

    def swap(i):
        part = pl.ds(i * quarter, quarter)
        return pltpu.make_async_remote_copy(
            src_ref=tokens_ref.at[part], dst_ref=incoming.at[part],
            send_sem=swap_send.at[i], recv_sem=swap_recv.at[i],
            device_id=partner, device_id_type=MESH,
        )

    @pl.when(moved)
    def _():
        swap(0).start()
        swap(1).start()

    meta_copy = pltpu.make_async_remote_copy(
        src_ref=own_meta, dst_ref=peer_meta, send_sem=meta_send.at[0], recv_sem=meta_recv.at[0],
        device_id=(c_peer, mine), device_id_type=MESH,
    )

    def view(step, a, b, c, side):
        if step >= steps:
            part = out_tile // 2
            return w_out.at[step - steps, a, b, c, :, pl.ds(side * part, part)]
        part = rows // 2
        return weights.at[step, a, b, c, pl.ds(side * part, part), :]

    def everything(count):
        return pl.ds(0, count)

    def push(ref, send, recv, peer):
        return pltpu.make_async_remote_copy(
            src_ref=ref, dst_ref=ref, send_sem=send, recv_sem=recv,
            device_id=(peer, mine), device_id_type=MESH,
        )

    def own_loaded(step):
        for copy in loads(step):
            copy.wait()

    def phase1(step):
        own_loaded(step)
        for side, peers in ((0, a_peers), (1, b_peers)):
            for peer in peers:
                push(
                    view(step, at_a, at_b, at_c, side),
                    p1_send.at[step, side], p1_recv.at[step, side], peer,
                ).start()

    def phase1_size(step, side):
        if side == 0:
            return view(step, pl.ds(0, rows_a - 1), at_b, at_c, 0)
        return view(step, at_a, pl.ds(0, rows_b - 1), at_c, 1)

    def phase2(step):
        for peer in b_peers:
            push(
                view(step, everything(rows_a), at_b, at_c, 0),
                p2_send.at[step, 0], p2_recv.at[step, 0], peer,
            ).start()
        for peer in a_peers:
            push(
                view(step, at_a, everything(rows_b), at_c, 1),
                p2_send.at[step, 1], p2_recv.at[step, 1], peer,
            ).start()

    def phase2_size(step, side):
        if side == 0:
            return view(step, everything(rows_a), pl.ds(0, rows_b - 1), at_c, 0)
        return view(step, pl.ds(0, rows_a - 1), everything(rows_b), at_c, 1)

    def phase3(step):
        ref = w_out.at[step - steps, :, :, at_c] if step >= steps else weights.at[step, :, :, at_c]
        return push(ref, p3_send.at[step], p3_recv.at[step], c_peer)

    def drain(ref, sem):
        pltpu.make_async_copy(ref, ref, sem).wait()

    def wait1(step):
        for side in range(2):
            drain(phase1_size(step, side), p1_recv.at[step, side])

    def wait2(step):
        for side in range(2):
            drain(phase2_size(step, side), p2_recv.at[step, side])

    def forward(turn):
        if turn < total:
            wait1(turn)
            phase2(turn)
        if turn + 2 < total:
            phase1(turn + 2)
        if 0 < turn <= total:
            wait2(turn - 1)
            phase3(turn - 1).start()

    norm_tile = min(tok // 4, 64)

    def normalize(source, first, count):
        @pl.loop(0, count // norm_tile)
        def _(i):
            part = pl.ds(pl.multiple_of(first + i * norm_tile, norm_tile), norm_tile)
            resid = source[part, :].astype(jnp.float32)
            center = jnp.mean(resid, axis=-1, keepdims=True)
            centred = resid - center
            spread = jnp.mean(centred * centred, axis=-1, keepdims=True)
            value = centred * lax.rsqrt(spread + 1e-05) * gain_ref[...]
            normed[part, :] = value.astype(jnp.bfloat16)

    def receive_rows(piece):
        for i in (2 * piece, 2 * piece + 1):
            swap(i).wait_recv()
        normalize(incoming, piece * 2 * quarter, 2 * quarter)

    phase1(0)
    phase1(1)
    meta_copy.start()

    @pl.when(kept)
    def _():
        normalize(tokens_ref, 0, tok)

    piece_rows = tok // 2
    row_head = lax.broadcasted_iota(jnp.int32, (LANES, LANES), 0) // head_size
    col_head = lax.broadcasted_iota(jnp.int32, (LANES, LANES), 1) // head_size
    same_head = (row_head == col_head).astype(jnp.float32).astype(jnp.bfloat16)

    def unit(x):
        square = x * x
        high = square.astype(jnp.bfloat16)
        low = (square - high.astype(jnp.float32)).astype(jnp.bfloat16)
        total = jnp.dot(high, same_head, preferred_element_type=jnp.float32)
        total += jnp.dot(low, same_head, preferred_element_type=jnp.float32)
        return (x * lax.rsqrt(total + 1e-06)).astype(jnp.bfloat16)

    def rows_of(piece):
        return pl.ds(pl.multiple_of(piece * piece_rows, piece_rows), piece_rows)

    def exchange(step, piece):
        part = rows_of(piece)
        return pltpu.make_async_remote_copy(
            src_ref=sent.at[step, :, part], dst_ref=held.at[pair_of(step), member, :, part],
            send_sem=a2a_send.at[step, piece], recv_sem=a2a_recv.at[pair_of(step), member, piece],
            device_id=device_of_member(group_of(step)), device_id_type=MESH,
        )

    def exchange_own(step, piece):
        part = rows_of(piece)
        return pltpu.make_async_copy(
            sent.at[step, :, part], held.at[pair_of(step), member, :, part],
            a2a_recv.at[pair_of(step), member, piece],
        )

    def project(step, piece):
        part = rows_of(piece)
        w = weights[step].reshape(width, 3 * LANES)
        y = jnp.dot(normed[part, :], w, preferred_element_type=jnp.float32)
        sent[step, 0, part, :] = unit(y[:, 0:LANES])
        sent[step, 1, part, :] = unit(y[:, LANES : 2 * LANES])
        sent[step, 2, part, :] = y[:, 2 * LANES :].astype(jnp.bfloat16)
        own = group_of(step) == member

        @pl.when(own)
        def _():
            exchange_own(step, piece).start()

        @pl.when(jnp.logical_not(own))
        def _():
            exchange(step, piece).start()

    early, late = steps // 4, steps - 2

    def project_turn(ready):
        if ready == early - 1:
            @pl.when(moved)
            def _():
                swap(0).wait_send()
                swap(2).start()
                swap(1).wait_send()
                swap(3).start()
        if ready == early:
            @pl.when(moved)
            def _():
                receive_rows(0)
        if ready == late:
            @pl.when(moved)
            def _():
                receive_rows(1)
        if ready < early:
            count = jnp.where(kept, 2, 0)
        elif ready == early:
            count = jnp.where(kept, 2, early + 1)
        elif ready < late:
            count = jnp.where(kept, 2, 1)
        elif ready == late:
            count = jnp.where(kept, 2, late + 2)
        else:
            count = 2

        @pl.loop(0, count)
        def _(i):
            if ready == early:
                step, piece = jnp.where(kept, ready, i), jnp.where(kept, i, 0)
            elif ready == late:
                step = jnp.where(kept, ready, (i + late) % (late + 1))
                piece = jnp.where(kept, i, jnp.minimum(i, 1))
            else:
                step, piece = ready, i
            project(step, piece)

    for turn in range(steps + 1):
        forward(turn)
        if turn > 0:
            phase3(turn - 1).wait_recv()
            project_turn(turn - 1)

    meta_copy.wait_recv()

    def first_of(block):
        where = pl.ds(block, 1)
        return jnp.where(kept, own_meta[where, :], peer_meta[where, :])

    def prepare(pair, block):
        where = pl.ds(pl.multiple_of(block * tok, tok), tok)
        spot = first_of(block) + lax.broadcasted_iota(jnp.int32, (1, tok), 1).astype(jnp.float32)
        region = (spot >= 0.0).astype(jnp.float32)
        row = lax.broadcasted_iota(jnp.int32, (LANES, tok), 0)
        feature = jnp.where(row == 0, region - 1.0, jnp.where(row == 1, -region, 0.0)) * FAR
        keys_t[pair, 0:LANES, where] = held[pair, block, 1].T
        keys_t[pair, LANES : 2 * LANES, where] = feature.astype(jnp.bfloat16)
        values_1[pair, where, 0:LANES] = held[pair, block, 2]
        values_1[pair, where, LANES : 2 * LANES] = jnp.ones((tok, LANES), jnp.bfloat16)

    def prepare_all(pair):
        for i in range(groups):
            block = (member + i) % groups
            for piece in range(2):
                part = rows_of(piece)
                drain(held.at[pair, block, :, part], a2a_recv.at[pair, block, piece])
            prepare(pair, block)

    lane = lax.broadcasted_iota(jnp.int32, (1, LANES), 1)
    pick = [
        (lane // head_size == hh).astype(jnp.float32).astype(jnp.bfloat16)
        for hh in range(LANES // head_size)
    ]
    tile = min(tok, 256)

    def attend(pair, block, target):
        base = first_of(block)[:, 0:LANES]

        @pl.loop(0, tok // tile)
        def _(i):
            start = pl.multiple_of(i * tile, tile)
            part = pl.ds(start, tile)
            spot = base + (start + lax.broadcasted_iota(jnp.int32, (tile, LANES), 0)).astype(jnp.float32)
            region = (spot >= 0.0).astype(jnp.float32)
            column = lax.broadcasted_iota(jnp.int32, (tile, LANES), 1)
            feature = jnp.where(column == 0, region, jnp.where(column == 1, 1.0 - region, 0.0))
            feature = feature.astype(jnp.bfloat16)
            query = held[pair, block, 0, part, :]
            result = None
            for hh, chosen in enumerate(pick):
                factor = scale_ref[member * group_heads + pair * len(pick) + hh] * math.log2(math.e)
                q = jnp.concatenate([query * chosen, feature], axis=1)
                score = jnp.dot(q, keys_t[pair], preferred_element_type=jnp.float32)
                best = jnp.max(score, axis=1, keepdims=True)
                weight = jnp.exp2((score - best) * factor).astype(jnp.bfloat16)
                both = jnp.dot(weight, values_1[pair], preferred_element_type=jnp.float32)
                o = both[:, 0:LANES] / both[:, LANES : 2 * LANES]
                result = o if result is None else jnp.where(column // head_size == hh, o, result)
            target[part, :] = result.astype(jnp.bfloat16)

    def block_at(k):
        return (half + 1 - k // depth) % 2 * depth + (place + 1 + k) % depth

    def is_home(k):
        return jnp.logical_and(kept, block_at(k) == mine)

    def give_back(pair, k):
        return pltpu.make_async_remote_copy(
            src_ref=heads_out.at[pair, k], dst_ref=attended.at[member, pair],
            send_sem=back_send.at[pair, k], recv_sem=back_recv.at[pair, member],
            device_id=home_of(block_at(k)), device_id_type=MESH,
        )

    def give_own(pair, k):
        return pltpu.make_async_copy(
            heads_out.at[pair, k], attended.at[member, pair], back_recv.at[pair, member]
        )

    turn = steps + 1
    for pair in range(pairs):
        prepare_all(pair)
        for k in range(groups):
            attend(pair, block_at(k), heads_out.at[pair, k])

            @pl.when(is_home(k))
            def _():
                give_own(pair, k).start()

            @pl.when(jnp.logical_not(is_home(k)))
            def _():
                give_back(pair, k).start()

            forward(turn)
            turn += 1
    while turn <= total:
        forward(turn)
        turn += 1

    for pair in range(pairs):
        for m in range(groups):
            drain(attended.at[m, pair], back_recv.at[pair, m])
    for chunk in range(chunks):
        phase3(steps + chunk).wait_recv()

    inner = groups * cols

    @pl.loop(0, chunks)
    def _(i):
        window = pl.ds(pl.multiple_of(i * out_tile, out_tile), out_tile)
        w = w_out[i].reshape(inner, out_tile)
        x = jnp.concatenate(
            [attended[g, pair] for g in range(groups) for pair in range(pairs)], axis=1
        )
        y = jnp.dot(x, w, preferred_element_type=jnp.float32)
        out_ref[:, window] = (tokens_ref[:, window].astype(jnp.float32) + y).astype(jnp.bfloat16)

    for step in range(total):
        for side in range(2):
            drain(phase1_size(step, side), p1_send.at[step, side])
            drain(phase2_size(step, side), p2_send.at[step, side])
        phase3(step).wait_send()
    meta_copy.wait_send()

    @pl.when(moved)
    def _():
        swap(2).wait_send()
        swap(3).wait_send()

    for step in range(steps):
        @pl.when(group_of(step) != member)
        def _():
            for piece in range(2):
                exchange(step, piece).wait_send()
    for pair in range(pairs):
        for k in range(groups):
            @pl.when(jnp.logical_not(is_home(k)))
            def _():
                give_back(pair, k).wait_send()


def per_device(tokens, block_map, shift, ln_gain, w_query, w_key, w_value, w_out, logit_scale):
    tok, width = tokens.shape
    heads = logit_scale.shape[0]
    inner = w_query.shape[1]
    head_size = inner // heads
    members = lax.axis_size("fsdp")
    groups = lax.axis_size("win")
    chips = members // 2
    rows_b = 2 ** ((chips.bit_length() - 1) // 2)
    rows_a = chips // rows_b
    pairs = inner // groups // LANES
    steps = groups * pairs
    total = steps + CHUNKS
    rows = w_query.shape[0]
    out_rows = w_out.shape[0]
    vmem = pl.BlockSpec(memory_space=pltpu.VMEM)
    smem = pl.BlockSpec(memory_space=pltpu.SMEM)
    far = pl.BlockSpec(memory_space=pl.ANY)
    dma = pltpu.SemaphoreType.DMA
    bf16 = jnp.bfloat16
    return pl.pallas_call(
        functools.partial(layer_kernel, (rows_a, rows_b, groups, head_size, pairs)),
        out_shape=jax.ShapeDtypeStruct((tok, width), bf16),
        in_specs=[vmem, smem, smem, vmem, far, far, far, far, smem],
        out_specs=vmem,
        scratch_shapes=[
            pltpu.VMEM((steps, rows_a, rows_b, 2, rows, 3 * LANES), bf16),
            pltpu.VMEM((CHUNKS, rows_a, rows_b, 2, out_rows, width // CHUNKS), bf16),
            pltpu.VMEM((tok, width), bf16),
            pltpu.VMEM((tok, width), bf16),
            pltpu.VMEM((steps, 3, tok, LANES), bf16),
            pltpu.VMEM((pairs, groups, 3, tok, LANES), bf16),
            pltpu.VMEM((pairs, 2 * LANES, groups * tok), bf16),
            pltpu.VMEM((pairs, groups * tok, 2 * LANES), bf16),
            pltpu.VMEM((pairs, groups, tok, LANES), bf16),
            pltpu.VMEM((groups, pairs, tok, LANES), bf16),
            pltpu.VMEM((8, tok), jnp.float32),
            pltpu.VMEM((8, tok), jnp.float32),
            dma((total, 3)),
            dma((total, 2)),
            dma((total, 2)),
            dma((total, 2)),
            dma((total, 2)),
            dma((total,)),
            dma((total,)),
            dma((4,)),
            dma((4,)),
            dma((1,)),
            dma((1,)),
            dma((steps, 2)),
            dma((pairs, groups, 2)),
            dma((pairs, groups)),
            dma((pairs, groups)),
        ],
        compiler_params=pltpu.CompilerParams(
            collective_id=0, has_side_effects=True, vmem_limit_bytes=60 * 1024 * 1024
        ),
    )(tokens, block_map, shift, ln_gain.reshape(1, width), w_query, w_key, w_value, w_out, logit_scale)


def solution(mesh):
    return jax.shard_map(
        per_device,
        mesh=mesh,
        in_specs=(
            P(("fsdp", "win"), None),
            P("fsdp", None),
            P("fsdp"),
            P(),
            P("fsdp", None),
            P("fsdp", None),
            P("fsdp", None),
            P("fsdp", None),
            P(),
        ),
        out_specs=P(("fsdp", "win"), None),
        check_vma=False,
    )
```

```python
import functools
import math

import jax
import jax.numpy as jnp
from jax import lax
from jax.experimental import pallas as pl
from jax.experimental.pallas import tpu as pltpu
from jax.sharding import PartitionSpec as P

MESH = pl.DeviceIdType.MESH
LANES = 128
FAR = 1024.0
CHUNKS = 4


def layer_kernel(
    sizes,
    tokens_ref, map_ref, shift_ref, gain_ref, wq_ref, wk_ref, wv_ref, wo_ref, scale_ref,
    out_ref,
    weights, w_out, incoming, normed, sent, held, keys_t, values_1, heads_out, attended, own_meta, peer_meta,
    load_sem, p1_send, p1_recv, p2_send, p2_recv, p3_send, p3_recv,
    swap_send, swap_recv, meta_send, meta_recv, a2a_send, a2a_recv, back_send, back_recv,
):
    rows_a, rows_b, groups, head_size, pairs = sizes
    tok, width = tokens_ref.shape
    rows = wq_ref.shape[0]
    cols = pairs * LANES
    group_heads = cols // head_size
    steps = groups * pairs
    chunks = w_out.shape[0]
    out_tile = w_out.shape[-1]
    total = steps + chunks
    me = lax.axis_index("fsdp")
    mine = lax.axis_index("win")
    chip = me // 2
    at_a = chip // rows_b
    at_b = chip % rows_b
    at_c = me % 2

    depth = groups // 2
    half = mine // depth
    place = mine % depth
    member = at_c * depth + place
    kept = at_c == half
    moved = at_c != half
    partner = (chip * 2 + 1 - at_c, (mine + depth) % groups)

    def device_of_member(m):
        return (chip * 2 + m // depth, half * depth + m % depth)

    def home_of(block):
        return (chip * 2 + half, block)

    def index_of(a, b, c):
        return (a * rows_b + b) * 2 + c

    a_peers = [index_of((at_a + i) % rows_a, at_b, at_c) for i in range(1, rows_a)]
    b_peers = [index_of(at_a, (at_b + i) % rows_b, at_c) for i in range(1, rows_b)]
    c_peer = index_of(at_a, at_b, 1 - at_c)

    barrier = pltpu.get_barrier_semaphore()
    greeted = 0
    for peer in a_peers + b_peers:
        pl.semaphore_signal(barrier, inc=1, device_id=(peer, mine), device_id_type=MESH)
        greeted += 1
    for core in range(2):
        for i in range(groups):
            if core or i:
                other = chip * 2 + (at_c + core) % 2
                pl.semaphore_signal(
                    barrier, inc=1, device_id=(other, (mine + i) % groups), device_id_type=MESH
                )
                greeted += 1

    def pair_of(step):
        return step % (steps // 2) // depth

    def group_of(step):
        return step % depth * depth + (place + 1 - step // (steps // 2)) % depth

    def loads(step):
        if step >= steps:
            chunk = step - steps
            return [
                pltpu.make_async_copy(
                    wo_ref.at[:, pl.ds(chunk * out_tile, out_tile)],
                    w_out.at[chunk, at_a, at_b, at_c],
                    load_sem.at[step, 0],
                )
            ]
        first = group_of(step) * cols + pair_of(step) * LANES
        window = pl.ds(pl.multiple_of(first, LANES), LANES)
        return [
            pltpu.make_async_copy(
                source.at[:, window],
                weights.at[step, at_a, at_b, at_c, :, pl.ds(m * LANES, LANES)],
                load_sem.at[step, m],
            )
            for m, source in enumerate((wq_ref, wk_ref, wv_ref))
        ]

    for step in range(total):
        for copy in loads(step):
            copy.start()
    for block in range(groups):
        first = (map_ref[0, block] * tok - shift_ref[0]).astype(jnp.float32)
        own_meta[block : block + 1, :] = jnp.full((1, tok), first, jnp.float32)
    own_meta[groups:, :] = jnp.zeros((own_meta.shape[0] - groups, tok), jnp.float32)
    pl.semaphore_wait(barrier, greeted)

    quarter = tok // 4

    def swap(i):
        part = pl.ds(i * quarter, quarter)
        return pltpu.make_async_remote_copy(
            src_ref=tokens_ref.at[part], dst_ref=incoming.at[part],
            send_sem=swap_send.at[i], recv_sem=swap_recv.at[i],
            device_id=partner, device_id_type=MESH,
        )

    @pl.when(moved)
    def _():
        swap(0).start()
        swap(1).start()

    meta_copy = pltpu.make_async_remote_copy(
        src_ref=own_meta, dst_ref=peer_meta, send_sem=meta_send.at[0], recv_sem=meta_recv.at[0],
        device_id=(c_peer, mine), device_id_type=MESH,
    )

    def view(step, a, b, c, side):
        if step >= steps:
            part = out_tile // 2
            return w_out.at[step - steps, a, b, c, :, pl.ds(side * part, part)]
        part = rows // 2
        return weights.at[step, a, b, c, pl.ds(side * part, part), :]

    def everything(count):
        return pl.ds(0, count)

    def push(ref, send, recv, peer):
        return pltpu.make_async_remote_copy(
            src_ref=ref, dst_ref=ref, send_sem=send, recv_sem=recv,
            device_id=(peer, mine), device_id_type=MESH,
        )

    def own_loaded(step):
        for copy in loads(step):
            copy.wait()

    def phase1(step):
        own_loaded(step)
        for side, peers in ((0, a_peers), (1, b_peers)):
            for peer in peers:
                push(
                    view(step, at_a, at_b, at_c, side),
                    p1_send.at[step, side], p1_recv.at[step, side], peer,
                ).start()

    def phase1_size(step, side):
        if side == 0:
            return view(step, pl.ds(0, rows_a - 1), at_b, at_c, 0)
        return view(step, at_a, pl.ds(0, rows_b - 1), at_c, 1)

    def phase2(step):
        for peer in b_peers:
            push(
                view(step, everything(rows_a), at_b, at_c, 0),
                p2_send.at[step, 0], p2_recv.at[step, 0], peer,
            ).start()
        for peer in a_peers:
            push(
                view(step, at_a, everything(rows_b), at_c, 1),
                p2_send.at[step, 1], p2_recv.at[step, 1], peer,
            ).start()

    def phase2_size(step, side):
        if side == 0:
            return view(step, everything(rows_a), pl.ds(0, rows_b - 1), at_c, 0)
        return view(step, pl.ds(0, rows_a - 1), everything(rows_b), at_c, 1)

    def phase3(step):
        ref = w_out.at[step - steps, :, :, at_c] if step >= steps else weights.at[step, :, :, at_c]
        return push(ref, p3_send.at[step], p3_recv.at[step], c_peer)

    def drain(ref, sem):
        pltpu.make_async_copy(ref, ref, sem).wait()

    def wait1(step):
        for side in range(2):
            drain(phase1_size(step, side), p1_recv.at[step, side])

    def wait2(step):
        for side in range(2):
            drain(phase2_size(step, side), p2_recv.at[step, side])

    def spread(step):
        if step < total:
            wait1(step)
            phase2(step)
        if step + 2 < total:
            phase1(step + 2)

    def pass_on(step):
        if 0 <= step < total:
            wait2(step)
            phase3(step).start()

    norm_tile = min(tok // 4, 64)

    def normalize(source, first, count):
        @pl.loop(0, count // norm_tile)
        def _(i):
            part = pl.ds(pl.multiple_of(first + i * norm_tile, norm_tile), norm_tile)
            resid = source[part, :].astype(jnp.float32)
            center = jnp.mean(resid, axis=-1, keepdims=True)
            centred = resid - center
            spread = jnp.mean(centred * centred, axis=-1, keepdims=True)
            value = centred * lax.rsqrt(spread + 1e-05) * gain_ref[...]
            normed[part, :] = value.astype(jnp.bfloat16)

    def receive_rows(piece):
        for i in (2 * piece, 2 * piece + 1):
            swap(i).wait_recv()
        normalize(incoming, piece * 2 * quarter, 2 * quarter)

    phase1(0)
    phase1(1)
    meta_copy.start()

    @pl.when(kept)
    def _():
        normalize(tokens_ref, 0, tok)

    piece_rows = tok // 2
    row_head = lax.broadcasted_iota(jnp.int32, (LANES, LANES), 0) // head_size
    col_head = lax.broadcasted_iota(jnp.int32, (LANES, LANES), 1) // head_size
    same_head = (row_head == col_head).astype(jnp.float32).astype(jnp.bfloat16)

    def unit(x):
        square = x * x
        high = square.astype(jnp.bfloat16)
        low = (square - high.astype(jnp.float32)).astype(jnp.bfloat16)
        total = jnp.dot(high, same_head, preferred_element_type=jnp.float32)
        total += jnp.dot(low, same_head, preferred_element_type=jnp.float32)
        return (x * lax.rsqrt(total + 1e-06)).astype(jnp.bfloat16)

    def rows_of(piece):
        return pl.ds(pl.multiple_of(piece * piece_rows, piece_rows), piece_rows)

    def exchange(step, piece):
        part = rows_of(piece)
        return pltpu.make_async_remote_copy(
            src_ref=sent.at[step, :, part], dst_ref=held.at[pair_of(step), member, :, part],
            send_sem=a2a_send.at[step, piece], recv_sem=a2a_recv.at[pair_of(step), member, piece],
            device_id=device_of_member(group_of(step)), device_id_type=MESH,
        )

    def exchange_own(step, piece):
        part = rows_of(piece)
        return pltpu.make_async_copy(
            sent.at[step, :, part], held.at[pair_of(step), member, :, part],
            a2a_recv.at[pair_of(step), member, piece],
        )

    def project_rows(step, part):
        w = weights[step].reshape(width, 3 * LANES)
        y = jnp.dot(normed[part, :], w, preferred_element_type=jnp.float32)
        sent[step, 0, part, :] = unit(y[:, 0:LANES])
        sent[step, 1, part, :] = unit(y[:, LANES : 2 * LANES])
        sent[step, 2, part, :] = y[:, 2 * LANES :].astype(jnp.bfloat16)

    def send_out(step, pieces):
        own = group_of(step) == member

        @pl.when(own)
        def _():
            for piece in pieces:
                exchange_own(step, piece).start()

        @pl.when(jnp.logical_not(own))
        def _():
            for piece in pieces:
                exchange(step, piece).start()

    def project(step, piece):
        project_rows(step, rows_of(piece))
        send_out(step, (piece,))

    early, late = steps // 4, steps - 3

    def project_turn(ready):
        if ready == early - 1:
            @pl.when(moved)
            def _():
                swap(2).start()
        if ready == early:
            @pl.when(moved)
            def _():
                swap(3).start()
                receive_rows(0)
        if ready < early:
            count = jnp.where(kept, 2, 0)
        elif ready == early:
            count = jnp.where(kept, 2, early + 1)
        else:
            count = jnp.where(kept, 2, 1)

        @pl.loop(0, count)
        def _(i):
            if ready == early:
                project(jnp.where(kept, ready, i), jnp.where(kept, i, 0))
            else:
                project(ready, i)

    for turn in range(late + 2):
        spread(turn)
        pass_on(turn - 1)
        if turn > 0:
            phase3(turn - 1).wait_recv()
            project_turn(turn - 1)

    spread(late + 2)

    @pl.when(moved)
    def _():
        receive_rows(1)

        @pl.loop(0, late + 1)
        def _(i):
            rest = (steps // 2 - depth) // 2 * 2
            step = jnp.where(i < depth, i, jnp.where(i < 2 * depth, i + rest, i - depth))
            project(step, 1)

    pass_on(late + 1)
    spread(late + 3)

    def project_last():
        for step in range(late + 1, steps):
            phase3(step).wait_recv()

        @pl.loop(late + 1, steps)
        def _(step):
            project_rows(step, pl.ds(0, tok))
            send_out(step, (0, 1))

    meta_copy.wait_recv()

    def first_of(block):
        where = pl.ds(block, 1)
        return jnp.where(kept, own_meta[where, :], peer_meta[where, :])

    def prepare(pair, block):
        where = pl.ds(pl.multiple_of(block * tok, tok), tok)
        spot = first_of(block) + lax.broadcasted_iota(jnp.int32, (1, tok), 1).astype(jnp.float32)
        region = (spot >= 0.0).astype(jnp.float32)
        row = lax.broadcasted_iota(jnp.int32, (LANES, tok), 0)
        feature = jnp.where(row == 0, region - 1.0, jnp.where(row == 1, -region, 0.0)) * FAR
        keys_t[pair, 0:LANES, where] = held[pair, block, 1].T
        keys_t[pair, LANES : 2 * LANES, where] = feature.astype(jnp.bfloat16)
        values_1[pair, where, 0:LANES] = held[pair, block, 2]
        values_1[pair, where, LANES : 2 * LANES] = jnp.ones((tok, LANES), jnp.bfloat16)

    def prepare_all(pair):
        for i in range(groups):
            block = (member + i) % groups
            for piece in range(2):
                part = rows_of(piece)
                drain(held.at[pair, block, :, part], a2a_recv.at[pair, block, piece])
            prepare(pair, block)

    lane = lax.broadcasted_iota(jnp.int32, (1, LANES), 1)
    pick = [
        (lane // head_size == hh).astype(jnp.float32).astype(jnp.bfloat16)
        for hh in range(LANES // head_size)
    ]

    def attend(pair, block, target):
        base = first_of(block)[:, 0:LANES]

        spot = base + lax.broadcasted_iota(jnp.int32, (tok, LANES), 0).astype(jnp.float32)
        region = (spot >= 0.0).astype(jnp.float32)
        column = lax.broadcasted_iota(jnp.int32, (tok, LANES), 1)
        feature = jnp.where(column == 0, region, jnp.where(column == 1, 1.0 - region, 0.0))
        feature = feature.astype(jnp.bfloat16)
        query = held[pair, block, 0]
        result = None
        for hh, chosen in enumerate(pick):
            factor = scale_ref[member * group_heads + pair * len(pick) + hh] * math.log2(math.e)
            q = jnp.concatenate([query * chosen, feature], axis=1)
            score = jnp.dot(q, keys_t[pair], preferred_element_type=jnp.float32)
            best = jnp.max(score, axis=1, keepdims=True)
            weight = jnp.exp2((score - best) * factor).astype(jnp.bfloat16)
            both = jnp.dot(weight, values_1[pair], preferred_element_type=jnp.float32)
            o = both[:, 0:LANES] / both[:, LANES : 2 * LANES]
            result = o if result is None else jnp.where(column // head_size == hh, o, result)
        target[...] = result.astype(jnp.bfloat16)

    def block_at(k):
        return (half + 1 - k // depth) % 2 * depth + (place + 1 + k) % depth

    def is_home(k):
        return jnp.logical_and(kept, block_at(k) == mine)

    def give_back(pair, k):
        return pltpu.make_async_remote_copy(
            src_ref=heads_out.at[pair, k], dst_ref=attended.at[member, pair],
            send_sem=back_send.at[pair, k], recv_sem=back_recv.at[pair, member],
            device_id=home_of(block_at(k)), device_id_type=MESH,
        )

    def give_own(pair, k):
        return pltpu.make_async_copy(
            heads_out.at[pair, k], attended.at[member, pair], back_recv.at[pair, member]
        )

    pass_on(late + 2)
    spread(late + 4)
    project_last()

    upcoming = list(range(late + 3, total))
    after = {(0, 0): 1, (0, 2): 1, (1, 0): 1, (1, 2): 1}
    for pair in range(pairs):
        prepare_all(pair)
        for k in range(groups):
            attend(pair, block_at(k), heads_out.at[pair, k])

            @pl.when(is_home(k))
            def _():
                give_own(pair, k).start()

            @pl.when(jnp.logical_not(is_home(k)))
            def _():
                give_back(pair, k).start()

            for _ in range(after.get((pair, k), 0)):
                if upcoming:
                    step = upcoming.pop(0)
                    pass_on(step)
                    spread(step + 2)
    for step in upcoming:
        pass_on(step)

    for pair in range(pairs):
        for m in range(groups):
            drain(attended.at[m, pair], back_recv.at[pair, m])
    for chunk in range(chunks):
        phase3(steps + chunk).wait_recv()

    inner = groups * cols

    @pl.loop(0, chunks)
    def _(i):
        window = pl.ds(pl.multiple_of(i * out_tile, out_tile), out_tile)
        w = w_out[i].reshape(inner, out_tile)
        x = jnp.concatenate(
            [attended[g, pair] for g in range(groups) for pair in range(pairs)], axis=1
        )
        y = jnp.dot(x, w, preferred_element_type=jnp.float32)
        out_ref[:, window] = (tokens_ref[:, window].astype(jnp.float32) + y).astype(jnp.bfloat16)

    for step in range(total):
        for side in range(2):
            drain(phase1_size(step, side), p1_send.at[step, side])
            drain(phase2_size(step, side), p2_send.at[step, side])
        phase3(step).wait_send()
    meta_copy.wait_send()

    @pl.when(moved)
    def _():
        for i in range(4):
            swap(i).wait_send()

    for step in range(steps):
        @pl.when(group_of(step) != member)
        def _():
            for piece in range(2):
                exchange(step, piece).wait_send()
    for pair in range(pairs):
        for k in range(groups):
            @pl.when(jnp.logical_not(is_home(k)))
            def _():
                give_back(pair, k).wait_send()


def per_device(tokens, block_map, shift, ln_gain, w_query, w_key, w_value, w_out, logit_scale):
    tok, width = tokens.shape
    heads = logit_scale.shape[0]
    inner = w_query.shape[1]
    head_size = inner // heads
    members = lax.axis_size("fsdp")
    groups = lax.axis_size("win")
    chips = members // 2
    rows_b = 2 ** ((chips.bit_length() - 1) // 2)
    rows_a = chips // rows_b
    pairs = inner // groups // LANES
    steps = groups * pairs
    total = steps + CHUNKS
    rows = w_query.shape[0]
    out_rows = w_out.shape[0]
    vmem = pl.BlockSpec(memory_space=pltpu.VMEM)
    smem = pl.BlockSpec(memory_space=pltpu.SMEM)
    far = pl.BlockSpec(memory_space=pl.ANY)
    dma = pltpu.SemaphoreType.DMA
    bf16 = jnp.bfloat16
    return pl.pallas_call(
        functools.partial(layer_kernel, (rows_a, rows_b, groups, head_size, pairs)),
        out_shape=jax.ShapeDtypeStruct((tok, width), bf16),
        in_specs=[vmem, smem, smem, vmem, far, far, far, far, smem],
        out_specs=vmem,
        scratch_shapes=[
            pltpu.VMEM((steps, rows_a, rows_b, 2, rows, 3 * LANES), bf16),
            pltpu.VMEM((CHUNKS, rows_a, rows_b, 2, out_rows, width // CHUNKS), bf16),
            pltpu.VMEM((tok, width), bf16),
            pltpu.VMEM((tok, width), bf16),
            pltpu.VMEM((steps, 3, tok, LANES), bf16),
            pltpu.VMEM((pairs, groups, 3, tok, LANES), bf16),
            pltpu.VMEM((pairs, 2 * LANES, groups * tok), bf16),
            pltpu.VMEM((pairs, groups * tok, 2 * LANES), bf16),
            pltpu.VMEM((pairs, groups, tok, LANES), bf16),
            pltpu.VMEM((groups, pairs, tok, LANES), bf16),
            pltpu.VMEM((8, tok), jnp.float32),
            pltpu.VMEM((8, tok), jnp.float32),
            dma((total, 3)),
            dma((total, 2)),
            dma((total, 2)),
            dma((total, 2)),
            dma((total, 2)),
            dma((total,)),
            dma((total,)),
            dma((4,)),
            dma((4,)),
            dma((1,)),
            dma((1,)),
            dma((steps, 2)),
            dma((pairs, groups, 2)),
            dma((pairs, groups)),
            dma((pairs, groups)),
        ],
        compiler_params=pltpu.CompilerParams(
            collective_id=0, has_side_effects=True, vmem_limit_bytes=60 * 1024 * 1024
        ),
    )(tokens, block_map, shift, ln_gain.reshape(1, width), w_query, w_key, w_value, w_out, logit_scale)


def solution(mesh):
    return jax.shard_map(
        per_device,
        mesh=mesh,
        in_specs=(
            P(("fsdp", "win"), None),
            P("fsdp", None),
            P("fsdp"),
            P(),
            P("fsdp", None),
            P("fsdp", None),
            P("fsdp", None),
            P("fsdp", None),
            P(),
        ),
        out_specs=P(("fsdp", "win"), None),
        check_vma=False,
    )
```

```python
import functools
import math

import jax
import jax.numpy as jnp
from jax import lax
from jax.experimental import pallas as pl
from jax.experimental.pallas import tpu as pltpu
from jax.sharding import PartitionSpec as P

MESH = pl.DeviceIdType.MESH
LANES = 128
FAR = 1024.0
CHUNKS = 4


def layer_kernel(
    sizes,
    tokens_ref, map_ref, shift_ref, gain_ref, wq_ref, wk_ref, wv_ref, wo_ref, scale_ref,
    out_ref,
    weights, w_out, incoming, normed, sent, held, keys_t, values_1, heads_out, attended, own_meta, peer_meta,
    load_sem, p1_send, p1_recv, p2_send, p2_recv, p3_send, p3_recv,
    swap_send, swap_recv, meta_send, meta_recv, a2a_send, a2a_recv, back_send, back_recv,
):
    rows_a, rows_b, groups, head_size, pairs = sizes
    tok, width = tokens_ref.shape
    rows = wq_ref.shape[0]
    cols = pairs * LANES
    group_heads = cols // head_size
    steps = groups * pairs
    chunks = w_out.shape[0]
    out_tile = w_out.shape[-1]
    total = steps + chunks
    me = lax.axis_index("fsdp")
    mine = lax.axis_index("win")
    chip = me // 2
    at_a = chip // rows_b
    at_b = chip % rows_b
    at_c = me % 2

    depth = groups // 2
    half = mine // depth
    place = mine % depth
    member = at_c * depth + place
    kept = at_c == half
    moved = at_c != half
    partner = (chip * 2 + 1 - at_c, (mine + depth) % groups)

    def device_of_member(m):
        return (chip * 2 + m // depth, half * depth + m % depth)

    def home_of(block):
        return (chip * 2 + half, block)

    def index_of(a, b, c):
        return (a * rows_b + b) * 2 + c

    a_peers = [index_of((at_a + i) % rows_a, at_b, at_c) for i in range(1, rows_a)]
    b_peers = [index_of(at_a, (at_b + i) % rows_b, at_c) for i in range(1, rows_b)]
    c_peer = index_of(at_a, at_b, 1 - at_c)

    barrier = pltpu.get_barrier_semaphore()
    greeted = 0
    for peer in a_peers + b_peers:
        pl.semaphore_signal(barrier, inc=1, device_id=(peer, mine), device_id_type=MESH)
        greeted += 1
    for core in range(2):
        for i in range(groups):
            if core or i:
                other = chip * 2 + (at_c + core) % 2
                pl.semaphore_signal(
                    barrier, inc=1, device_id=(other, (mine + i) % groups), device_id_type=MESH
                )
                greeted += 1

    def pair_of(step):
        return step % (steps // 2) // depth

    def group_of(step):
        return step % depth * depth + (place + 1 - step // (steps // 2)) % depth

    def loads(step):
        if step >= steps:
            chunk = step - steps
            return [
                pltpu.make_async_copy(
                    wo_ref.at[:, pl.ds(chunk * out_tile, out_tile)],
                    w_out.at[chunk, at_a, at_b, at_c],
                    load_sem.at[step, 0],
                )
            ]
        first = group_of(step) * cols + pair_of(step) * LANES
        window = pl.ds(pl.multiple_of(first, LANES), LANES)
        return [
            pltpu.make_async_copy(
                source.at[:, window],
                weights.at[step, at_a, at_b, at_c, :, pl.ds(m * LANES, LANES)],
                load_sem.at[step, m],
            )
            for m, source in enumerate((wq_ref, wk_ref, wv_ref))
        ]

    for step in range(total):
        for copy in loads(step):
            copy.start()
    for block in range(groups):
        first = (map_ref[0, block] * tok - shift_ref[0]).astype(jnp.float32)
        own_meta[block : block + 1, :] = jnp.full((1, tok), first, jnp.float32)
    own_meta[groups:, :] = jnp.zeros((own_meta.shape[0] - groups, tok), jnp.float32)
    pl.semaphore_wait(barrier, greeted)

    quarter = tok // 4

    def swap(i):
        part = pl.ds(i * quarter, quarter)
        return pltpu.make_async_remote_copy(
            src_ref=tokens_ref.at[part], dst_ref=incoming.at[part],
            send_sem=swap_send.at[i], recv_sem=swap_recv.at[i],
            device_id=partner, device_id_type=MESH,
        )

    @pl.when(moved)
    def _():
        swap(0).start()
        swap(1).start()

    meta_copy = pltpu.make_async_remote_copy(
        src_ref=own_meta, dst_ref=peer_meta, send_sem=meta_send.at[0], recv_sem=meta_recv.at[0],
        device_id=(c_peer, mine), device_id_type=MESH,
    )

    def view(step, a, b, c, side):
        if step >= steps:
            part = out_tile // 2
            return w_out.at[step - steps, a, b, c, :, pl.ds(side * part, part)]
        part = rows // 2
        return weights.at[step, a, b, c, pl.ds(side * part, part), :]

    def everything(count):
        return pl.ds(0, count)

    def push(ref, send, recv, peer):
        return pltpu.make_async_remote_copy(
            src_ref=ref, dst_ref=ref, send_sem=send, recv_sem=recv,
            device_id=(peer, mine), device_id_type=MESH,
        )

    def own_loaded(step):
        for copy in loads(step):
            copy.wait()

    def phase1(step):
        own_loaded(step)
        for side, peers in ((0, a_peers), (1, b_peers)):
            for peer in peers:
                push(
                    view(step, at_a, at_b, at_c, side),
                    p1_send.at[step, side], p1_recv.at[step, side], peer,
                ).start()

    def phase1_size(step, side):
        if side == 0:
            return view(step, pl.ds(0, rows_a - 1), at_b, at_c, 0)
        return view(step, at_a, pl.ds(0, rows_b - 1), at_c, 1)

    def phase2(step):
        for peer in b_peers:
            push(
                view(step, everything(rows_a), at_b, at_c, 0),
                p2_send.at[step, 0], p2_recv.at[step, 0], peer,
            ).start()
        for peer in a_peers:
            push(
                view(step, at_a, everything(rows_b), at_c, 1),
                p2_send.at[step, 1], p2_recv.at[step, 1], peer,
            ).start()

    def phase2_size(step, side):
        if side == 0:
            return view(step, everything(rows_a), pl.ds(0, rows_b - 1), at_c, 0)
        return view(step, pl.ds(0, rows_a - 1), everything(rows_b), at_c, 1)

    def phase3(step):
        ref = w_out.at[step - steps, :, :, at_c] if step >= steps else weights.at[step, :, :, at_c]
        return push(ref, p3_send.at[step], p3_recv.at[step], c_peer)

    def drain(ref, sem):
        pltpu.make_async_copy(ref, ref, sem).wait()

    def wait1(step):
        for side in range(2):
            drain(phase1_size(step, side), p1_recv.at[step, side])

    def wait2(step):
        for side in range(2):
            drain(phase2_size(step, side), p2_recv.at[step, side])

    def forward(turn):
        if turn < total:
            wait1(turn)
            phase2(turn)
        if turn + 2 < total:
            phase1(turn + 2)
        if 0 < turn <= total:
            wait2(turn - 1)
            phase3(turn - 1).start()

    norm_tile = min(tok // 4, 64)

    def normalize(source, first, count):
        @pl.loop(0, count // norm_tile)
        def _(i):
            part = pl.ds(pl.multiple_of(first + i * norm_tile, norm_tile), norm_tile)
            resid = source[part, :].astype(jnp.float32)
            center = jnp.mean(resid, axis=-1, keepdims=True)
            centred = resid - center
            spread = jnp.mean(centred * centred, axis=-1, keepdims=True)
            value = centred * lax.rsqrt(spread + 1e-05) * gain_ref[...]
            normed[part, :] = value.astype(jnp.bfloat16)

    def receive_rows(piece):
        for i in (2 * piece, 2 * piece + 1):
            swap(i).wait_recv()
        normalize(incoming, piece * 2 * quarter, 2 * quarter)

    phase1(0)
    phase1(1)
    meta_copy.start()

    @pl.when(kept)
    def _():
        normalize(tokens_ref, 0, tok)

    piece_rows = tok // 2
    row_head = lax.broadcasted_iota(jnp.int32, (LANES, LANES), 0) // head_size
    col_head = lax.broadcasted_iota(jnp.int32, (LANES, LANES), 1) // head_size
    same_head = (row_head == col_head).astype(jnp.float32).astype(jnp.bfloat16)

    def unit(x):
        square = x * x
        high = square.astype(jnp.bfloat16)
        low = (square - high.astype(jnp.float32)).astype(jnp.bfloat16)
        total = jnp.dot(high, same_head, preferred_element_type=jnp.float32)
        total += jnp.dot(low, same_head, preferred_element_type=jnp.float32)
        return (x * lax.rsqrt(total + 1e-06)).astype(jnp.bfloat16)

    def rows_of(piece):
        return pl.ds(pl.multiple_of(piece * piece_rows, piece_rows), piece_rows)

    def exchange(step, piece):
        part = rows_of(piece)
        return pltpu.make_async_remote_copy(
            src_ref=sent.at[step, :, part], dst_ref=held.at[pair_of(step), member, :, part],
            send_sem=a2a_send.at[step, piece], recv_sem=a2a_recv.at[pair_of(step), member, piece],
            device_id=device_of_member(group_of(step)), device_id_type=MESH,
        )

    def exchange_own(step, piece):
        part = rows_of(piece)
        return pltpu.make_async_copy(
            sent.at[step, :, part], held.at[pair_of(step), member, :, part],
            a2a_recv.at[pair_of(step), member, piece],
        )

    def project(step, piece):
        part = rows_of(piece)
        w = weights[step].reshape(width, 3 * LANES)
        y = jnp.dot(normed[part, :], w, preferred_element_type=jnp.float32)
        sent[step, 0, part, :] = unit(y[:, 0:LANES])
        sent[step, 1, part, :] = unit(y[:, LANES : 2 * LANES])
        sent[step, 2, part, :] = y[:, 2 * LANES :].astype(jnp.bfloat16)
        own = group_of(step) == member

        @pl.when(own)
        def _():
            exchange_own(step, piece).start()

        @pl.when(jnp.logical_not(own))
        def _():
            exchange(step, piece).start()

    early, late = steps // 4, steps - 2

    def project_turn(ready):
        if ready == early - 1:
            @pl.when(moved)
            def _():
                swap(0).wait_send()
                swap(2).start()
                swap(1).wait_send()
                swap(3).start()
        if ready == early:
            @pl.when(moved)
            def _():
                receive_rows(0)
        if ready == late:
            @pl.when(moved)
            def _():
                receive_rows(1)
        if ready < early:
            count = jnp.where(kept, 2, 0)
        elif ready == early:
            count = jnp.where(kept, 2, early + 1)
        elif ready < late:
            count = jnp.where(kept, 2, 1)
        elif ready == late:
            count = jnp.where(kept, 2, late + 2)
        else:
            count = 2

        @pl.loop(0, count)
        def _(i):
            if ready == early:
                step, piece = jnp.where(kept, ready, i), jnp.where(kept, i, 0)
            elif ready == late:
                step = jnp.where(kept, ready, (i + late) % (late + 1))
                piece = jnp.where(kept, i, jnp.minimum(i, 1))
            else:
                step, piece = ready, i
            project(step, piece)

    for turn in range(steps + 1):
        forward(turn)
        if turn > 0:
            phase3(turn - 1).wait_recv()
            project_turn(turn - 1)

    meta_copy.wait_recv()

    def first_of(block):
        where = pl.ds(block, 1)
        return jnp.where(kept, own_meta[where, :], peer_meta[where, :])

    def prepare(pair, block):
        where = pl.ds(pl.multiple_of(block * tok, tok), tok)
        spot = first_of(block) + lax.broadcasted_iota(jnp.int32, (1, tok), 1).astype(jnp.float32)
        region = (spot >= 0.0).astype(jnp.float32)
        row = lax.broadcasted_iota(jnp.int32, (LANES, tok), 0)
        feature = jnp.where(row == 0, region - 1.0, jnp.where(row == 1, -region, 0.0)) * FAR
        keys_t[pair, 0:LANES, where] = held[pair, block, 1].T
        keys_t[pair, LANES : 2 * LANES, where] = feature.astype(jnp.bfloat16)
        values_1[pair, where, 0:LANES] = held[pair, block, 2]
        values_1[pair, where, LANES : 2 * LANES] = jnp.ones((tok, LANES), jnp.bfloat16)

    def prepare_all(pair):
        for i in range(groups):
            block = (member + i) % groups
            for piece in range(2):
                part = rows_of(piece)
                drain(held.at[pair, block, :, part], a2a_recv.at[pair, block, piece])
            prepare(pair, block)

    lane = lax.broadcasted_iota(jnp.int32, (1, LANES), 1)
    pick = [
        (lane // head_size == hh).astype(jnp.float32).astype(jnp.bfloat16)
        for hh in range(LANES // head_size)
    ]

    def attend(pair, block, target):
        base = first_of(block)[:, 0:LANES]

        spot = base + lax.broadcasted_iota(jnp.int32, (tok, LANES), 0).astype(jnp.float32)
        region = (spot >= 0.0).astype(jnp.float32)
        column = lax.broadcasted_iota(jnp.int32, (tok, LANES), 1)
        feature = jnp.where(column == 0, region, jnp.where(column == 1, 1.0 - region, 0.0))
        feature = feature.astype(jnp.bfloat16)
        query = held[pair, block, 0]
        result = None
        for hh, chosen in enumerate(pick):
            factor = scale_ref[member * group_heads + pair * len(pick) + hh] * math.log2(math.e)
            q = jnp.concatenate([query * chosen, feature], axis=1)
            score = jnp.dot(q, keys_t[pair], preferred_element_type=jnp.float32)
            best = jnp.max(score, axis=1, keepdims=True)
            weight = jnp.exp2((score - best) * factor).astype(jnp.bfloat16)
            both = jnp.dot(weight, values_1[pair], preferred_element_type=jnp.float32)
            o = both[:, 0:LANES] / both[:, LANES : 2 * LANES]
            result = o if result is None else jnp.where(column // head_size == hh, o, result)
        target[...] = result.astype(jnp.bfloat16)

    def block_at(k):
        return (half + 1 - k // depth) % 2 * depth + (place + 1 + k) % depth

    def is_home(k):
        return jnp.logical_and(kept, block_at(k) == mine)

    def give_back(pair, k):
        return pltpu.make_async_remote_copy(
            src_ref=heads_out.at[pair, k], dst_ref=attended.at[member, pair],
            send_sem=back_send.at[pair, k], recv_sem=back_recv.at[pair, member],
            device_id=home_of(block_at(k)), device_id_type=MESH,
        )

    def give_own(pair, k):
        return pltpu.make_async_copy(
            heads_out.at[pair, k], attended.at[member, pair], back_recv.at[pair, member]
        )

    first_turn = steps + 1

    @pl.loop(0, pairs * groups)
    def _(i):
        pair, k = i // groups, i % groups

        @pl.when(k == 0)
        def _():
            prepare_all(pair)

        attend(pair, block_at(k), heads_out.at[pair, k])

        @pl.when(is_home(k))
        def _():
            give_own(pair, k).start()

        @pl.when(jnp.logical_not(is_home(k)))
        def _():
            give_back(pair, k).start()

        for turn in range(first_turn, min(total + 1, first_turn + pairs * groups)):
            @pl.when(i == turn - first_turn)
            def _():
                forward(turn)

    for turn in range(first_turn + pairs * groups, total + 1):
        forward(turn)

    for pair in range(pairs):
        for m in range(groups):
            drain(attended.at[m, pair], back_recv.at[pair, m])
    for chunk in range(chunks):
        phase3(steps + chunk).wait_recv()

    inner = groups * cols

    @pl.loop(0, chunks)
    def _(i):
        window = pl.ds(pl.multiple_of(i * out_tile, out_tile), out_tile)
        w = w_out[i].reshape(inner, out_tile)
        x = jnp.concatenate(
            [attended[g, pair] for g in range(groups) for pair in range(pairs)], axis=1
        )
        y = jnp.dot(x, w, preferred_element_type=jnp.float32)
        out_ref[:, window] = (tokens_ref[:, window].astype(jnp.float32) + y).astype(jnp.bfloat16)

    for step in range(total):
        for side in range(2):
            drain(phase1_size(step, side), p1_send.at[step, side])
            drain(phase2_size(step, side), p2_send.at[step, side])
        phase3(step).wait_send()
    meta_copy.wait_send()

    @pl.when(moved)
    def _():
        swap(2).wait_send()
        swap(3).wait_send()

    for step in range(steps):
        @pl.when(group_of(step) != member)
        def _():
            for piece in range(2):
                exchange(step, piece).wait_send()
    for pair in range(pairs):
        for k in range(groups):
            @pl.when(jnp.logical_not(is_home(k)))
            def _():
                give_back(pair, k).wait_send()


def per_device(tokens, block_map, shift, ln_gain, w_query, w_key, w_value, w_out, logit_scale):
    tok, width = tokens.shape
    heads = logit_scale.shape[0]
    inner = w_query.shape[1]
    head_size = inner // heads
    members = lax.axis_size("fsdp")
    groups = lax.axis_size("win")
    chips = members // 2
    rows_b = 2 ** ((chips.bit_length() - 1) // 2)
    rows_a = chips // rows_b
    pairs = inner // groups // LANES
    steps = groups * pairs
    total = steps + CHUNKS
    rows = w_query.shape[0]
    out_rows = w_out.shape[0]
    vmem = pl.BlockSpec(memory_space=pltpu.VMEM)
    smem = pl.BlockSpec(memory_space=pltpu.SMEM)
    far = pl.BlockSpec(memory_space=pl.ANY)
    dma = pltpu.SemaphoreType.DMA
    bf16 = jnp.bfloat16
    return pl.pallas_call(
        functools.partial(layer_kernel, (rows_a, rows_b, groups, head_size, pairs)),
        out_shape=jax.ShapeDtypeStruct((tok, width), bf16),
        in_specs=[vmem, smem, smem, vmem, far, far, far, far, smem],
        out_specs=vmem,
        scratch_shapes=[
            pltpu.VMEM((steps, rows_a, rows_b, 2, rows, 3 * LANES), bf16),
            pltpu.VMEM((CHUNKS, rows_a, rows_b, 2, out_rows, width // CHUNKS), bf16),
            pltpu.VMEM((tok, width), bf16),
            pltpu.VMEM((tok, width), bf16),
            pltpu.VMEM((steps, 3, tok, LANES), bf16),
            pltpu.VMEM((pairs, groups, 3, tok, LANES), bf16),
            pltpu.VMEM((pairs, 2 * LANES, groups * tok), bf16),
            pltpu.VMEM((pairs, groups * tok, 2 * LANES), bf16),
            pltpu.VMEM((pairs, groups, tok, LANES), bf16),
            pltpu.VMEM((groups, pairs, tok, LANES), bf16),
            pltpu.VMEM((8, tok), jnp.float32),
            pltpu.VMEM((8, tok), jnp.float32),
            dma((total, 3)),
            dma((total, 2)),
            dma((total, 2)),
            dma((total, 2)),
            dma((total, 2)),
            dma((total,)),
            dma((total,)),
            dma((4,)),
            dma((4,)),
            dma((1,)),
            dma((1,)),
            dma((steps, 2)),
            dma((pairs, groups, 2)),
            dma((pairs, groups)),
            dma((pairs, groups)),
        ],
        compiler_params=pltpu.CompilerParams(
            collective_id=0, has_side_effects=True, vmem_limit_bytes=60 * 1024 * 1024
        ),
    )(tokens, block_map, shift, ln_gain.reshape(1, width), w_query, w_key, w_value, w_out, logit_scale)


def solution(mesh):
    return jax.shard_map(
        per_device,
        mesh=mesh,
        in_specs=(
            P(("fsdp", "win"), None),
            P("fsdp", None),
            P("fsdp"),
            P(),
            P("fsdp", None),
            P("fsdp", None),
            P("fsdp", None),
            P("fsdp", None),
            P(),
        ),
        out_specs=P(("fsdp", "win"), None),
        check_vma=False,
    )
```

```python
import functools
import math

import jax
import jax.numpy as jnp
from jax import lax
from jax.experimental import pallas as pl
from jax.experimental.pallas import tpu as pltpu
from jax.sharding import PartitionSpec as P

MESH = pl.DeviceIdType.MESH
LANES = 128
FAR = 1024.0
CHUNKS = 4


def layer_kernel(
    sizes,
    tokens_ref, map_ref, shift_ref, gain_ref, wq_ref, wk_ref, wv_ref, wo_ref, scale_ref,
    out_ref,
    weights, w_out, incoming, normed, sent, held, keys_t, values_1, heads_out, attended, own_meta, peer_meta,
    load_sem, p1_send, p1_recv, p2_send, p2_recv, p3_send, p3_recv,
    swap_send, swap_recv, meta_send, meta_recv, a2a_send, a2a_recv, back_send, back_recv,
):
    rows_a, rows_b, groups, head_size, pairs = sizes
    tok, width = tokens_ref.shape
    rows = wq_ref.shape[0]
    cols = pairs * LANES
    group_heads = cols // head_size
    steps = groups * pairs
    chunks = w_out.shape[0]
    out_tile = w_out.shape[-1]
    total = steps + chunks
    me = lax.axis_index("fsdp")
    mine = lax.axis_index("win")
    chip = me // 2
    at_a = chip // rows_b
    at_b = chip % rows_b
    at_c = me % 2

    depth = groups // 2
    half = mine // depth
    place = mine % depth
    member = at_c * depth + place
    kept = at_c == half
    moved = at_c != half
    partner = (chip * 2 + 1 - at_c, (mine + depth) % groups)

    def device_of_member(m):
        return (chip * 2 + m // depth, half * depth + m % depth)

    def home_of(block):
        return (chip * 2 + half, block)

    def index_of(a, b, c):
        return (a * rows_b + b) * 2 + c

    a_peers = [index_of((at_a + i) % rows_a, at_b, at_c) for i in range(1, rows_a)]
    b_peers = [index_of(at_a, (at_b + i) % rows_b, at_c) for i in range(1, rows_b)]
    c_peer = index_of(at_a, at_b, 1 - at_c)

    barrier = pltpu.get_barrier_semaphore()
    greeted = 0
    for peer in a_peers + b_peers:
        pl.semaphore_signal(barrier, inc=1, device_id=(peer, mine), device_id_type=MESH)
        greeted += 1
    for core in range(2):
        for i in range(groups):
            if core or i:
                other = chip * 2 + (at_c + core) % 2
                pl.semaphore_signal(
                    barrier, inc=1, device_id=(other, (mine + i) % groups), device_id_type=MESH
                )
                greeted += 1

    def pair_of(step):
        return step % (steps // 2) // depth

    def group_of(step):
        return step % depth * depth + (place + 1 - step // (steps // 2)) % depth

    def loads(step):
        if step >= steps:
            chunk = step - steps
            return [
                pltpu.make_async_copy(
                    wo_ref.at[:, pl.ds(chunk * out_tile, out_tile)],
                    w_out.at[chunk, at_a, at_b, at_c],
                    load_sem.at[step, 0],
                )
            ]
        first = group_of(step) * cols + pair_of(step) * LANES
        window = pl.ds(pl.multiple_of(first, LANES), LANES)
        return [
            pltpu.make_async_copy(
                source.at[:, window],
                weights.at[step, at_a, at_b, at_c, :, pl.ds(m * LANES, LANES)],
                load_sem.at[step, m],
            )
            for m, source in enumerate((wq_ref, wk_ref, wv_ref))
        ]

    for step in range(total):
        for copy in loads(step):
            copy.start()
    for block in range(groups):
        first = (map_ref[0, block] * tok - shift_ref[0]).astype(jnp.float32)
        own_meta[block : block + 1, :] = jnp.full((1, tok), first, jnp.float32)
    own_meta[groups:, :] = jnp.zeros((own_meta.shape[0] - groups, tok), jnp.float32)
    pl.semaphore_wait(barrier, greeted)

    quarter = tok // 4

    def swap(i):
        part = pl.ds(i * quarter, quarter)
        return pltpu.make_async_remote_copy(
            src_ref=tokens_ref.at[part], dst_ref=incoming.at[part],
            send_sem=swap_send.at[i], recv_sem=swap_recv.at[i],
            device_id=partner, device_id_type=MESH,
        )

    @pl.when(moved)
    def _():
        swap(0).start()
        swap(1).start()

    meta_copy = pltpu.make_async_remote_copy(
        src_ref=own_meta, dst_ref=peer_meta, send_sem=meta_send.at[0], recv_sem=meta_recv.at[0],
        device_id=(c_peer, mine), device_id_type=MESH,
    )

    def view(step, a, b, c, side):
        if step >= steps:
            part = out_tile // 2
            return w_out.at[step - steps, a, b, c, :, pl.ds(side * part, part)]
        part = rows // 2
        return weights.at[step, a, b, c, pl.ds(side * part, part), :]

    def everything(count):
        return pl.ds(0, count)

    def push(ref, send, recv, peer):
        return pltpu.make_async_remote_copy(
            src_ref=ref, dst_ref=ref, send_sem=send, recv_sem=recv,
            device_id=(peer, mine), device_id_type=MESH,
        )

    def own_loaded(step):
        for copy in loads(step):
            copy.wait()

    def phase1(step):
        own_loaded(step)
        for side, peers in ((0, a_peers), (1, b_peers)):
            for peer in peers:
                push(
                    view(step, at_a, at_b, at_c, side),
                    p1_send.at[step, side], p1_recv.at[step, side], peer,
                ).start()

    def phase1_size(step, side):
        if side == 0:
            return view(step, pl.ds(0, rows_a - 1), at_b, at_c, 0)
        return view(step, at_a, pl.ds(0, rows_b - 1), at_c, 1)

    def phase2(step):
        for peer in b_peers:
            push(
                view(step, everything(rows_a), at_b, at_c, 0),
                p2_send.at[step, 0], p2_recv.at[step, 0], peer,
            ).start()
        for peer in a_peers:
            push(
                view(step, at_a, everything(rows_b), at_c, 1),
                p2_send.at[step, 1], p2_recv.at[step, 1], peer,
            ).start()

    def phase2_size(step, side):
        if side == 0:
            return view(step, everything(rows_a), pl.ds(0, rows_b - 1), at_c, 0)
        return view(step, pl.ds(0, rows_a - 1), everything(rows_b), at_c, 1)

    def phase3(step):
        ref = w_out.at[step - steps, :, :, at_c] if step >= steps else weights.at[step, :, :, at_c]
        return push(ref, p3_send.at[step], p3_recv.at[step], c_peer)

    def drain(ref, sem):
        pltpu.make_async_copy(ref, ref, sem).wait()

    def wait1(step):
        for side in range(2):
            drain(phase1_size(step, side), p1_recv.at[step, side])

    def wait2(step):
        for side in range(2):
            drain(phase2_size(step, side), p2_recv.at[step, side])

    def spread(step):
        if step < total:
            wait1(step)
            phase2(step)
        if step + 2 < total:
            phase1(step + 2)

    def pass_on(step):
        if 0 <= step < total:
            wait2(step)
            phase3(step).start()

    norm_tile = min(tok // 4, 64)

    def normalize(source, first, count):
        @pl.loop(0, count // norm_tile)
        def _(i):
            part = pl.ds(pl.multiple_of(first + i * norm_tile, norm_tile), norm_tile)
            resid = source[part, :].astype(jnp.float32)
            center = jnp.mean(resid, axis=-1, keepdims=True)
            centred = resid - center
            spread = jnp.mean(centred * centred, axis=-1, keepdims=True)
            value = centred * lax.rsqrt(spread + 1e-05) * gain_ref[...]
            normed[part, :] = value.astype(jnp.bfloat16)

    def receive_rows(piece):
        for i in (2 * piece, 2 * piece + 1):
            swap(i).wait_recv()
        normalize(incoming, piece * 2 * quarter, 2 * quarter)

    phase1(0)
    phase1(1)
    meta_copy.start()

    @pl.when(kept)
    def _():
        normalize(tokens_ref, 0, tok)

    piece_rows = tok // 2
    row_head = lax.broadcasted_iota(jnp.int32, (LANES, LANES), 0) // head_size
    col_head = lax.broadcasted_iota(jnp.int32, (LANES, LANES), 1) // head_size
    same_head = (row_head == col_head).astype(jnp.float32).astype(jnp.bfloat16)

    def unit(x):
        square = x * x
        high = square.astype(jnp.bfloat16)
        low = (square - high.astype(jnp.float32)).astype(jnp.bfloat16)
        total = jnp.dot(high, same_head, preferred_element_type=jnp.float32)
        total += jnp.dot(low, same_head, preferred_element_type=jnp.float32)
        return (x * lax.rsqrt(total + 1e-06)).astype(jnp.bfloat16)

    def rows_of(piece):
        return pl.ds(pl.multiple_of(piece * piece_rows, piece_rows), piece_rows)

    def exchange(step, piece):
        part = rows_of(piece)
        return pltpu.make_async_remote_copy(
            src_ref=sent.at[step, :, part], dst_ref=held.at[pair_of(step), member, :, part],
            send_sem=a2a_send.at[step, piece], recv_sem=a2a_recv.at[pair_of(step), member, piece],
            device_id=device_of_member(group_of(step)), device_id_type=MESH,
        )

    def exchange_own(step, piece):
        part = rows_of(piece)
        return pltpu.make_async_copy(
            sent.at[step, :, part], held.at[pair_of(step), member, :, part],
            a2a_recv.at[pair_of(step), member, piece],
        )

    def project_rows(step, part):
        w = weights[step].reshape(width, 3 * LANES)
        y = jnp.dot(normed[part, :], w, preferred_element_type=jnp.float32)
        sent[step, 0, part, :] = unit(y[:, 0:LANES])
        sent[step, 1, part, :] = unit(y[:, LANES : 2 * LANES])
        sent[step, 2, part, :] = y[:, 2 * LANES :].astype(jnp.bfloat16)

    def send_out(step, pieces):
        own = group_of(step) == member

        @pl.when(own)
        def _():
            for piece in pieces:
                exchange_own(step, piece).start()

        @pl.when(jnp.logical_not(own))
        def _():
            for piece in pieces:
                exchange(step, piece).start()

    def project(step, piece):
        project_rows(step, rows_of(piece))
        send_out(step, (piece,))

    early, late = steps // 4, steps - 3

    def project_turn(ready):
        if ready == early - 1:
            @pl.when(moved)
            def _():
                swap(2).start()
        if ready == early:
            @pl.when(moved)
            def _():
                swap(3).start()
                receive_rows(0)
        if ready < early:
            count = jnp.where(kept, 2, 0)
        elif ready == early:
            count = jnp.where(kept, 2, early + 1)
        else:
            count = jnp.where(kept, 2, 1)

        @pl.loop(0, count)
        def _(i):
            if ready == early:
                project(jnp.where(kept, ready, i), jnp.where(kept, i, 0))
            else:
                project(ready, i)

    for turn in range(late + 2):
        spread(turn)
        pass_on(turn - 1)
        if turn > 0:
            phase3(turn - 1).wait_recv()
            project_turn(turn - 1)

    spread(late + 2)

    @pl.when(moved)
    def _():
        receive_rows(1)

        @pl.loop(0, late + 1)
        def _(i):
            rest = (steps // 2 - depth) // 2 * 2
            step = jnp.where(i < depth, i, jnp.where(i < 2 * depth, i + rest, i - depth))
            project(step, 1)

    pass_on(late + 1)
    spread(late + 3)

    def project_last():
        for step in range(late + 1, steps):
            phase3(step).wait_recv()

        @pl.loop(late + 1, steps)
        def _(step):
            project_rows(step, pl.ds(0, tok))
            send_out(step, (0, 1))

    meta_copy.wait_recv()

    def first_of(block):
        where = pl.ds(block, 1)
        return jnp.where(kept, own_meta[where, :], peer_meta[where, :])

    def prepare(pair, block):
        where = pl.ds(pl.multiple_of(block * tok, tok), tok)
        spot = first_of(block) + lax.broadcasted_iota(jnp.int32, (1, tok), 1).astype(jnp.float32)
        region = (spot >= 0.0).astype(jnp.float32)
        row = lax.broadcasted_iota(jnp.int32, (LANES, tok), 0)
        feature = jnp.where(row == 0, region - 1.0, jnp.where(row == 1, -region, 0.0)) * FAR
        keys_t[pair, 0:LANES, where] = held[pair, block, 1].T
        keys_t[pair, LANES : 2 * LANES, where] = feature.astype(jnp.bfloat16)
        values_1[pair, where, 0:LANES] = held[pair, block, 2]
        values_1[pair, where, LANES : 2 * LANES] = jnp.ones((tok, LANES), jnp.bfloat16)

    def prepare_all(pair):
        for i in range(groups):
            block = (member + i) % groups
            for piece in range(2):
                part = rows_of(piece)
                drain(held.at[pair, block, :, part], a2a_recv.at[pair, block, piece])
            prepare(pair, block)

    lane = lax.broadcasted_iota(jnp.int32, (1, LANES), 1)
    pick = [
        (lane // head_size == hh).astype(jnp.float32).astype(jnp.bfloat16)
        for hh in range(LANES // head_size)
    ]

    def attend(pair, block, target):
        base = first_of(block)[:, 0:LANES]

        spot = base + lax.broadcasted_iota(jnp.int32, (tok, LANES), 0).astype(jnp.float32)
        region = (spot >= 0.0).astype(jnp.float32)
        column = lax.broadcasted_iota(jnp.int32, (tok, LANES), 1)
        feature = jnp.where(column == 0, region, jnp.where(column == 1, 1.0 - region, 0.0))
        feature = feature.astype(jnp.bfloat16)
        query = held[pair, block, 0]
        result = None
        for hh, chosen in enumerate(pick):
            factor = scale_ref[member * group_heads + pair * len(pick) + hh] * math.log2(math.e)
            q = jnp.concatenate([query * chosen, feature], axis=1)
            score = jnp.dot(q, keys_t[pair], preferred_element_type=jnp.float32)
            best = jnp.max(score, axis=1, keepdims=True)
            weight = jnp.exp2((score - best) * factor).astype(jnp.bfloat16)
            both = jnp.dot(weight, values_1[pair], preferred_element_type=jnp.float32)
            o = both[:, 0:LANES] / both[:, LANES : 2 * LANES]
            result = o if result is None else jnp.where(column // head_size == hh, o, result)
        target[...] = result.astype(jnp.bfloat16)

    def block_at(k):
        return (half + 1 - k // depth) % 2 * depth + (place + 1 + k) % depth

    def is_home(k):
        return jnp.logical_and(kept, block_at(k) == mine)

    def give_back(pair, k):
        return pltpu.make_async_remote_copy(
            src_ref=heads_out.at[pair, k], dst_ref=attended.at[member, pair],
            send_sem=back_send.at[pair, k], recv_sem=back_recv.at[pair, member],
            device_id=home_of(block_at(k)), device_id_type=MESH,
        )

    def give_own(pair, k):
        return pltpu.make_async_copy(
            heads_out.at[pair, k], attended.at[member, pair], back_recv.at[pair, member]
        )

    pass_on(late + 2)
    spread(late + 4)
    project_last()

    @pl.loop(0, pairs * groups)
    def _(i):
        pair, k = i // groups, i % groups

        @pl.when(k == 0)
        def _():
            prepare_all(pair)

        attend(pair, block_at(k), heads_out.at[pair, k])

        @pl.when(is_home(k))
        def _():
            give_own(pair, k).start()

        @pl.when(jnp.logical_not(is_home(k)))
        def _():
            give_back(pair, k).start()

        for n, step in enumerate(range(late + 3, total)):
            @pl.when(i == 2 * n)
            def _():
                pass_on(step)
                spread(step + 2)

    for pair in range(pairs):
        for m in range(groups):
            drain(attended.at[m, pair], back_recv.at[pair, m])
    for chunk in range(chunks):
        phase3(steps + chunk).wait_recv()

    inner = groups * cols

    @pl.loop(0, chunks)
    def _(i):
        window = pl.ds(pl.multiple_of(i * out_tile, out_tile), out_tile)
        w = w_out[i].reshape(inner, out_tile)
        x = jnp.concatenate(
            [attended[g, pair] for g in range(groups) for pair in range(pairs)], axis=1
        )
        y = jnp.dot(x, w, preferred_element_type=jnp.float32)
        out_ref[:, window] = (tokens_ref[:, window].astype(jnp.float32) + y).astype(jnp.bfloat16)

    for step in range(total):
        for side in range(2):
            drain(phase1_size(step, side), p1_send.at[step, side])
            drain(phase2_size(step, side), p2_send.at[step, side])
        phase3(step).wait_send()
    meta_copy.wait_send()

    @pl.when(moved)
    def _():
        for i in range(4):
            swap(i).wait_send()

    for step in range(steps):
        @pl.when(group_of(step) != member)
        def _():
            for piece in range(2):
                exchange(step, piece).wait_send()
    for pair in range(pairs):
        for k in range(groups):
            @pl.when(jnp.logical_not(is_home(k)))
            def _():
                give_back(pair, k).wait_send()


def per_device(tokens, block_map, shift, ln_gain, w_query, w_key, w_value, w_out, logit_scale):
    tok, width = tokens.shape
    heads = logit_scale.shape[0]
    inner = w_query.shape[1]
    head_size = inner // heads
    members = lax.axis_size("fsdp")
    groups = lax.axis_size("win")
    chips = members // 2
    rows_b = 2 ** ((chips.bit_length() - 1) // 2)
    rows_a = chips // rows_b
    pairs = inner // groups // LANES
    steps = groups * pairs
    total = steps + CHUNKS
    rows = w_query.shape[0]
    out_rows = w_out.shape[0]
    vmem = pl.BlockSpec(memory_space=pltpu.VMEM)
    smem = pl.BlockSpec(memory_space=pltpu.SMEM)
    far = pl.BlockSpec(memory_space=pl.ANY)
    dma = pltpu.SemaphoreType.DMA
    bf16 = jnp.bfloat16
    return pl.pallas_call(
        functools.partial(layer_kernel, (rows_a, rows_b, groups, head_size, pairs)),
        out_shape=jax.ShapeDtypeStruct((tok, width), bf16),
        in_specs=[vmem, smem, smem, vmem, far, far, far, far, smem],
        out_specs=vmem,
        scratch_shapes=[
            pltpu.VMEM((steps, rows_a, rows_b, 2, rows, 3 * LANES), bf16),
            pltpu.VMEM((CHUNKS, rows_a, rows_b, 2, out_rows, width // CHUNKS), bf16),
            pltpu.VMEM((tok, width), bf16),
            pltpu.VMEM((tok, width), bf16),
            pltpu.VMEM((steps, 3, tok, LANES), bf16),
            pltpu.VMEM((pairs, groups, 3, tok, LANES), bf16),
            pltpu.VMEM((pairs, 2 * LANES, groups * tok), bf16),
            pltpu.VMEM((pairs, groups * tok, 2 * LANES), bf16),
            pltpu.VMEM((pairs, groups, tok, LANES), bf16),
            pltpu.VMEM((groups, pairs, tok, LANES), bf16),
            pltpu.VMEM((8, tok), jnp.float32),
            pltpu.VMEM((8, tok), jnp.float32),
            dma((total, 3)),
            dma((total, 2)),
            dma((total, 2)),
            dma((total, 2)),
            dma((total, 2)),
            dma((total,)),
            dma((total,)),
            dma((4,)),
            dma((4,)),
            dma((1,)),
            dma((1,)),
            dma((steps, 2)),
            dma((pairs, groups, 2)),
            dma((pairs, groups)),
            dma((pairs, groups)),
        ],
        compiler_params=pltpu.CompilerParams(
            collective_id=0, has_side_effects=True, vmem_limit_bytes=60 * 1024 * 1024
        ),
    )(tokens, block_map, shift, ln_gain.reshape(1, width), w_query, w_key, w_value, w_out, logit_scale)


def solution(mesh):
    return jax.shard_map(
        per_device,
        mesh=mesh,
        in_specs=(
            P(("fsdp", "win"), None),
            P("fsdp", None),
            P("fsdp"),
            P(),
            P("fsdp", None),
            P("fsdp", None),
            P("fsdp", None),
            P("fsdp", None),
            P(),
        ),
        out_specs=P(("fsdp", "win"), None),
        check_vma=False,
    )
```
